32 devices in a mesh: ctx: 4 (over z), seq: 8 (over y, x, core).
Axes of the slice: x: 2, y: 2, z: 4, core: 2. Of those that a mesh axis runs over, the one named last changes fastest.
Arguments:
- queries: bfloat16 [8192, 128], P(('seq', 'ctx')), may hold values from -6 to 6
- keys: bfloat16 [8192, 128], P(('seq', 'ctx')), may hold values from -6 to 6
- values: bfloat16 [8192, 1024], P(('seq', 'ctx')), may hold values from -6 to 6
- grad_output: bfloat16 [8192, 1024], P(('seq', 'ctx')), may hold values from -6 to 6
Outputs:
- attended: bfloat16 [8192, 1024], P(('seq', 'ctx'))
- grad_queries: bfloat16 [8192, 128], P(('seq', 'ctx'))
- grad_keys: bfloat16 [8192, 128], P(('seq', 'ctx'))
- grad_values: bfloat16 [8192, 1024], P(('seq', 'ctx'))
The draws below stay inside these ranges and needn't reach their ends.
All inputs are finite; a program needn't handle non-finite values.
Results may differ from the reference program's by a relative error of at most 0.001.
Values sent between devices are 32-bit elements; how exact they have to be, the bound alone decides.
A program may use at most 128 MiB of HBM per device.

```python
import math
import jax
import jax.numpy as jnp
import numpy as np
from jax import lax

HEADS = 8
QK_DIM = 16
HEAD_DIM = 128
TOK_DEV = 256
FEATURES = 153
TOKENS = 8192


def levels(stream_key, dims, cuts, low, top_value):
    def one(dim, blocks):
        draws = jax.random.uniform(jax.random.fold_in(jax.random.fold_in(stream_key, 6), dim), (blocks,), jnp.float32, low / len(cuts), top_value / len(cuts))
        return jnp.repeat(jnp.exp(draws), dims[dim] // blocks).reshape((-1,) + (1,) * (len(dims) - dim - 1))

    level = one(*cuts[0])
    for cut in cuts[1:]:
        level = level * one(*cut)
    return level


def normal_values(stream_key, shape, scale, bound, cuts=(), kind=jnp.bfloat16):
    values = scale * jax.random.normal(stream_key, shape, jnp.float32)
    if cuts:
        values = values * levels(stream_key, shape, cuts, -0.22, 0.18)
    return jnp.clip(values, -bound, bound).astype(kind)


def setup_inputs(seed: int = 0) -> dict:
    streams_of = jax.random.split(jax.random.key(seed), 5)
    queries = normal_values(streams_of[0], (TOKENS, HEADS * QK_DIM), 1.0, 6.0, ((0, 32),))
    keys = normal_values(streams_of[1], (TOKENS, HEADS * QK_DIM), 1.0, 6.0, ((0, 32),))
    values = normal_values(streams_of[2], (TOKENS, HEADS * HEAD_DIM), 1.0, 6.0, ((0, 32),))
    grad_output = normal_values(streams_of[3], (TOKENS, HEADS * HEAD_DIM), 1.0, 6.0, ((0, 32),))
    return {"queries": queries, "keys": keys, "values": values, "grad_output": grad_output}


HIGHEST = lax.Precision.HIGHEST

def features(entries):
    width = entries.shape[1]
    upper, lower = np.triu_indices(width)
    factors = np.where(upper == lower, 1.0, math.sqrt(2.0)) / math.sqrt(2.0 * width)
    ones = jnp.ones_like(entries[:, :1, :])
    linear = entries / math.sqrt(math.sqrt(width))
    square = entries[:, upper, :] * entries[:, lower, :] * jnp.asarray(factors, entries.dtype)[None, :, None]
    return jnp.concatenate([ones, linear, square], axis=1)

def block_kernel(query, key_rows):
    length = query.shape[0]
    query_half = query.astype(jnp.bfloat16)
    key_half = key_rows.astype(jnp.bfloat16)
    dots = jnp.einsum('thd,shd->hts', query_half, key_half, preferred_element_type=jnp.float32) / math.sqrt(query.shape[-1])
    causal = jnp.arange(length)[:, None] >= jnp.arange(length)[None, :]
    kernel = jnp.where(causal[None], 1.0 + dots + 0.5 * dots * dots, 0.0)
    return (dots, kernel, causal)

def forward_block(left, kernel, value, prior_state, prior_norm):
    numer = jnp.einsum('hts,she->the', kernel, value, precision=HIGHEST)
    numer = numer + jnp.einsum('hft,hfe->the', left, prior_state, precision=HIGHEST)
    denom = lax.optimization_barrier(jnp.sum(kernel, axis=-1)).T + jnp.einsum('hft,hf->th', left, prior_norm, precision=HIGHEST)
    output = numer / denom[:, :, None]
    return (output, denom)

def later_terms(left, grad, output, denom):
    scaled = grad / denom[:, :, None]
    share = lax.optimization_barrier(jnp.sum(grad * output, axis=-1)) / denom
    term_state = jnp.einsum('hft,the->hfe', left, scaled, precision=HIGHEST)
    term_norm = jnp.einsum('hft,th->hf', left, share, precision=HIGHEST)
    return (scaled, share, term_state, term_norm)

def backward_block(query, key_rows, value, scaled, share, dots, kernel, causal, right, left_pull, right_pull, prior_state, prior_norm, later_state, later_norm):
    direct = jnp.einsum('the,she->hts', scaled, value, precision=HIGHEST) - share.T[:, :, None]
    grad_kernel = jnp.where(causal[None], direct, 0.0)
    grad_left = jnp.einsum('hfe,the->hft', prior_state, scaled, precision=HIGHEST) - prior_norm[:, :, None] * share.T[:, None, :]
    grad_right = jnp.einsum('hfe,she->hfs', later_state, value, precision=HIGHEST) - later_norm[:, :, None]
    grad_value = jnp.einsum('hts,the->she', kernel, scaled, precision=HIGHEST)
    grad_value = grad_value + jnp.einsum('hfs,hfe->she', right, later_state, precision=HIGHEST)
    grad_dots = grad_kernel * (1.0 + dots) / math.sqrt(query.shape[-1])
    grad_query = jnp.einsum('hts,shd->thd', grad_dots, key_rows, precision=HIGHEST)
    grad_query = grad_query + jnp.transpose(left_pull(grad_left)[0], (2, 0, 1))
    grad_key = jnp.einsum('hts,thd->shd', grad_dots, query, precision=HIGHEST)
    grad_key = grad_key + jnp.transpose(right_pull(grad_right)[0], (2, 0, 1))
    return (grad_query, grad_key, grad_value)

def reference(queries, keys, values, grad_output):
    blocks = TOKENS // TOK_DEV

    def split(array, width):
        return array.astype(jnp.float32).reshape(blocks, TOK_DEV, HEADS, width)
    query_blocks = split(queries, QK_DIM)
    key_blocks = split(keys, QK_DIM)
    value_blocks = split(values, HEAD_DIM)
    grad_blocks = split(grad_output, HEAD_DIM)

    def forward_step(carry, inputs):
        prior_state, prior_norm = carry
        query, key_rows, value, grad = inputs
        left = features(jnp.transpose(query, (1, 2, 0)))
        right = features(jnp.transpose(key_rows, (1, 2, 0)))
        dots, kernel, causal = block_kernel(query, key_rows)
        output, denom = forward_block(left, kernel, value, prior_state, prior_norm)
        scaled, share, term_state, term_norm = later_terms(left, grad, output, denom)
        state = jnp.einsum('hfs,she->hfe', right, value, precision=HIGHEST)
        norm = lax.optimization_barrier(jnp.sum(right, axis=-1))
        return ((prior_state + state, prior_norm + norm), (output, denom, prior_state, prior_norm, term_state, term_norm))
    start = (jnp.zeros((HEADS, FEATURES, HEAD_DIM), jnp.float32), jnp.zeros((HEADS, FEATURES), jnp.float32))
    final, stored = lax.scan(forward_step, start, (query_blocks, key_blocks, value_blocks, grad_blocks))
    outputs, denoms, prior_states, prior_norms, term_states, term_norms = stored

    def suffix_step(carry, inputs):
        return ((carry[0] + inputs[0], carry[1] + inputs[1]), carry)
    final_later, later = lax.scan(suffix_step, start, (term_states, term_norms), reverse=True)
    later_states, later_norms = later

    def backward_one(inputs):
        query, key_rows, value, grad, output, denom, prior_state, prior_norm, later_state, later_norm = inputs
        left, left_pull = jax.vjp(features, jnp.transpose(query, (1, 2, 0)))
        right, right_pull = jax.vjp(features, jnp.transpose(key_rows, (1, 2, 0)))
        dots, kernel, causal = block_kernel(query, key_rows)
        scaled, share, term_state, term_norm = later_terms(left, grad, output, denom)
        return backward_block(query, key_rows, value, scaled, share, dots, kernel, causal, right, left_pull, right_pull, prior_state, prior_norm, later_state, later_norm)
    grad_query, grad_key, grad_value = lax.map(backward_one, (query_blocks, key_blocks, value_blocks, grad_blocks, outputs, denoms, prior_states, prior_norms, later_states, later_norms))
    attended = outputs.reshape(TOKENS, HEADS * HEAD_DIM).astype(jnp.bfloat16)
    return (attended, grad_query.reshape(TOKENS, HEADS * QK_DIM).astype(jnp.bfloat16), grad_key.reshape(TOKENS, HEADS * QK_DIM).astype(jnp.bfloat16), grad_value.reshape(TOKENS, HEADS * HEAD_DIM).astype(jnp.bfloat16))
```

```python
import functools
import math

import jax
import jax.numpy as jnp
import numpy as np
from jax import lax
from jax.experimental import pallas as pl
from jax.experimental.pallas import tpu as pltpu
from jax.sharding import PartitionSpec as P

HEADS = 8
QK_DIM = 16
HEAD_DIM = 128
FEATURES = 153
ROWS = 160
LANES = 128
MESH = pl.DeviceIdType.MESH
NN = (((1,), (0,)), ((), ()))
NT = (((1,), (1,)), ((), ()))
TN = (((0,), (0,)), ((), ()))


def tables():
    upper, lower = np.triu_indices(QK_DIM)
    pick_a = np.zeros((HEADS, ROWS, LANES), np.float32)
    pick_b = np.zeros((HEADS, ROWS, LANES), np.float32)
    aux = np.zeros((8, ROWS), np.float32)
    aux[0, 0] = 1.0
    aux[1, : 1 + QK_DIM] = 1.0
    aux[2, 0] = 1.0
    aux[2, 1 : 1 + QK_DIM] = 1.0 / math.sqrt(math.sqrt(QK_DIM))
    aux[2, 1 + QK_DIM : FEATURES] = np.where(upper == lower, 1.0, math.sqrt(2.0)) / math.sqrt(
        2.0 * QK_DIM
    )
    for head in range(HEADS):
        base = head * QK_DIM
        for i in range(QK_DIM):
            pick_a[head, 1 + i, base + i] = 1.0
        for n, (i, j) in enumerate(zip(upper, lower)):
            pick_a[head, 1 + QK_DIM + n, base + i] = 1.0
            pick_b[head, 1 + QK_DIM + n, base + j] = 1.0
    aux_column = np.zeros((ROWS, LANES), np.float32)
    aux_column[:, :8] = aux.T
    return (
        jnp.asarray(pick_a, jnp.bfloat16),
        jnp.asarray(pick_b, jnp.bfloat16),
        jnp.asarray(aux),
        jnp.asarray(aux_column),
    )


def dot(a, b, dims=NN):
    return lax.dot_general(a, b, dims, preferred_element_type=jnp.float32)


def split(x):
    high = x.astype(jnp.bfloat16)
    return high, (x - high.astype(jnp.float32)).astype(jnp.bfloat16)


def dot2(pair, b, dims=NN):
    return dot(pair[0], b, dims) + dot(pair[1], b, dims)


def dot2r(a, pair, dims=NN):
    return dot(a, pair[0], dims) + dot(a, pair[1], dims)


def dot3(x, y, dims=NN):
    return dot(x[0], y[0], dims) + (dot(x[0], y[1], dims) + dot(x[1], y[0], dims))


def features_by_row(pick_a, pick_b, aux_column, x):
    a = dot(pick_a, x, NT) + aux_column[:, 0:1]
    b = dot(pick_b, x, NT) + aux_column[:, 1:2]
    return a * b * aux_column[:, 2:3]


def factors_by_token(pick_a, pick_b, aux, x):
    a = dot(x, pick_a, NT) + aux[0:1, :]
    b = dot(x, pick_b, NT) + aux[1:2, :]
    return a, b


def put_state(ref, state, norm):
    ref[0] = state
    ref[0, FEATURES : FEATURES + 1, :] = norm[0:1, :LANES]
    ref[0, FEATURES + 1 : FEATURES + 2, : ROWS - LANES] = norm[0:1, LANES:ROWS]


def norm_of(ref):
    return jnp.concatenate(
        [
            ref[0, FEATURES : FEATURES + 1, :],
            ref[0, FEATURES + 1 : FEATURES + 2, : ROWS - LANES],
        ],
        axis=1,
    )


def key_state_kernel(k_ref, v_ref, a_ref, b_ref, auxc_ref, x_ref):
    phi = split(features_by_row(a_ref[0], b_ref[0], auxc_ref, k_ref[...]))
    ones = jnp.ones((8, k_ref.shape[0]), jnp.bfloat16)
    put_state(x_ref, dot2(phi, v_ref[...]), dot2r(ones, phi, NT))


def pull(grad, a, b, pick_a, pick_b):
    return dot2(split(grad * b), pick_a) + dot2(split(grad * a), pick_b)


def middle_kernel(
    q_ref, k_ref, v_ref, g_ref, p_ref, a_ref, b_ref, aux_ref, auxc_ref,
    out_ref, gq_ref, x_ref, gk_ref, gv_ref, gq_acc, gk_acc,
):
    head = pl.program_id(0)
    length = q_ref.shape[0]
    q, k, v, g = q_ref[...], k_ref[...], v_ref[...], g_ref[...]
    pick_a, pick_b = a_ref[0], b_ref[0]
    scale = 1.0 / math.sqrt(QK_DIM)
    mine = lax.broadcasted_iota(jnp.int32, (length, LANES), 1) // QK_DIM == head
    q_mine = jnp.where(mine, q, jnp.zeros_like(q))
    k_mine = jnp.where(mine, k, jnp.zeros_like(k))
    s = dot(q_mine, k, NT) * scale
    causal = lax.broadcasted_iota(jnp.int32, (length, length), 0) >= lax.broadcasted_iota(
        jnp.int32, (length, length), 1
    )
    kern = split(jnp.where(causal, 1.0 + s + 0.5 * s * s, 0.0))
    local = dot2(kern, jnp.concatenate([v, jnp.ones_like(v)], axis=1))
    a, b = factors_by_token(pick_a, pick_b, aux_ref, q)
    phi = a * b * aux_ref[2:3, :]
    prior = split(p_ref[0])
    prior_norm = norm_of(p_ref)
    den = local[:, HEAD_DIM:] + jnp.sum(phi * prior_norm, axis=1, keepdims=True)
    rden = 1.0 / den
    out = (local[:, :HEAD_DIM] + dot3(split(phi), prior)) * rden
    out_ref[...] = out.astype(jnp.bfloat16)
    g32 = g.astype(jnp.float32)
    scaled = split(g32 * rden)
    weighed = g32 * out * rden
    share = jnp.sum(weighed, axis=1, keepdims=True)
    share_row = split(dot2r(jnp.ones((8, LANES), jnp.bfloat16), split(weighed), NT))
    phi_row = split(features_by_row(pick_a, pick_b, auxc_ref, q))
    put_state(x_ref, dot3(phi_row, scaled), dot3(share_row, phi_row, NT))
    rden_column = rden[:, 0:1]
    direct = dot(g, v, NT) * rden_column - share
    grad_dots = split(jnp.where(causal, direct * (1.0 + s) * scale, 0.0))
    gv_ref[...] = dot3(kern, scaled, TN)
    grad_phi = dot2r(g, prior, NT) * rden_column - share * prior_norm
    grad_q = dot2(grad_dots, k_mine) + pull(grad_phi * aux_ref[2:3, :], a, b, pick_a, pick_b)
    grad_k = dot2(grad_dots, q_mine, TN)

    @pl.when(head == 0)
    def _():
        gq_acc[...] = grad_q
        gk_acc[...] = grad_k

    @pl.when(head > 0)
    def _():
        gq_acc[...] += grad_q
        gk_acc[...] += grad_k

    @pl.when(head == HEADS - 1)
    def _():
        gq_ref[...] = gq_acc[...].astype(jnp.bfloat16)
        gk_ref[...] = gk_acc[...]


def last_kernel(
    k_ref, v_ref, l_ref, gk_in, gv_in, a_ref, b_ref, aux_ref, gk_ref, gv_ref, gk_acc
):
    head = pl.program_id(0)
    k, v = k_ref[...], v_ref[...]
    pick_a, pick_b = a_ref[0], b_ref[0]
    later = split(l_ref[0])
    later_norm = norm_of(l_ref)
    a, b = factors_by_token(pick_a, pick_b, aux_ref, k)
    factor = aux_ref[2:3, :]
    gv_ref[...] = (gv_in[...] + dot3(split(a * b * factor), later)).astype(jnp.bfloat16)
    grad_phi = dot2r(v, later, NT) - later_norm
    grad_k = pull(grad_phi * factor, a, b, pick_a, pick_b)

    @pl.when(head == 0)
    def _():
        gk_acc[...] = gk_in[...] + grad_k

    @pl.when(head > 0)
    def _():
        gk_acc[...] += grad_k

    @pl.when(head == HEADS - 1)
    def _():
        gk_ref[...] = gk_acc[...].astype(jnp.bfloat16)


def scan_kernel(
    n_ctx, n_seq, reverse, x_ref, p_ref, got, tot, before, up, down,
    send_sem, recv_sem,
):
    rounds = n_seq.bit_length() - 1
    chunks = x_ref.shape[0]
    up_at, down_at = rounds, rounds + 1
    ctx, seq = lax.axis_index("ctx"), lax.axis_index("seq")
    if reverse:
        place, line = n_ctx - 1 - ctx, n_seq - 1 - seq
        step = -1
    else:
        place, line = ctx, seq
        step = 1
    high = [(line // (1 << r)) % 2 for r in range(rounds)]
    partner = [seq + step * (1 << r) * (1 - 2 * high[r]) for r in range(rounds)]
    has_above = place < n_ctx - 1
    has_below = place > 0
    above = lax.rem(ctx + step + n_ctx, n_ctx)
    below = lax.rem(ctx - step + n_ctx, n_ctx)

    barrier = pltpu.get_barrier_semaphore()
    for r in range(rounds):
        pl.semaphore_signal(barrier, inc=1, device_id=(ctx, partner[r]), device_id_type=MESH)

    @pl.when(has_above)
    def _():
        pl.semaphore_signal(barrier, inc=1, device_id=(above, seq), device_id_type=MESH)

    @pl.when(has_below)
    def _():
        pl.semaphore_signal(barrier, inc=1, device_id=(below, seq), device_id_type=MESH)

    pl.semaphore_wait(
        barrier, rounds + (place + n_ctx - 1) // n_ctx + (n_ctx - 1 - place + n_ctx - 1) // n_ctx
    )

    def copy(stage, c, source, device):
        return pltpu.make_async_remote_copy(
            src_ref=source,
            dst_ref=got.at[stage, c],
            send_sem=send_sem.at[stage, c],
            recv_sem=recv_sem.at[stage, c],
            device_id=device,
            device_id_type=MESH,
        )

    def exchange(r, c):
        source = x_ref.at[c] if r == 0 else tot.at[r - 1, c]
        return copy(r, c, source, (ctx, partner[r]))

    def upward(c):
        return copy(up_at, c, up.at[c], (above, seq))

    def downward(c):
        return copy(down_at, c, down.at[c], (below, seq))

    def begin(r, c):
        if r < rounds:
            if r > 0:
                exchange(r - 1, c).wait_recv()
                arrived = got[r - 1, c]
                add = jnp.where(high[r - 1] == 1, arrived, 0.0)
                if r == 1:
                    before[c] = add
                    tot[0, c] = x_ref[c] + arrived
                else:
                    before[c] += add
                    tot[r - 1, c] = tot[r - 2, c] + arrived
            exchange(r, c).start()
        elif r == rounds:
            exchange(r - 1, c).wait_recv()
            add = jnp.where(high[r - 1] == 1, got[r - 1, c], 0.0)
            before[c] = before[c] + add if rounds > 1 else add

            @pl.when(has_above & ~has_below)
            def _():
                up[c] = before[c] + x_ref[c]
                upward(c).start()

            @pl.when(has_below & ~has_above)
            def _():
                down[c] = before[c]
                downward(c).start()
        else:
            @pl.when(has_below)
            def _():
                upward(c).wait_recv()

                @pl.when(has_above)
                def _():
                    up[c] = before[c] + x_ref[c] + got[up_at, c]
                    upward(c).start()

            @pl.when(has_above)
            def _():
                downward(c).wait_recv()

                @pl.when(has_below)
                def _():
                    down[c] = before[c] + got[down_at, c]
                    downward(c).start()

            p_ref[c] = before[c]

            @pl.when(has_below)
            def _():
                p_ref[c] += got[up_at, c]

            @pl.when(has_above)
            def _():
                p_ref[c] += got[down_at, c]

    lag = 2
    for turn in range(chunks + lag * (rounds + 1)):
        for r in reversed(range(rounds + 2)):
            c = turn - lag * r
            if 0 <= c < chunks:
                begin(r, c)

    for c in range(chunks):
        for r in range(rounds):
            exchange(r, c).wait_send()

        @pl.when(has_above)
        def _():
            upward(c).wait_send()

        @pl.when(has_below)
        def _():
            downward(c).wait_send()


def scan(x, n_ctx, n_seq, reverse):
    rounds = n_seq.bit_length() - 1
    shape = x.shape
    vmem = pl.BlockSpec(memory_space=pltpu.VMEM)
    return pl.pallas_call(
        functools.partial(scan_kernel, n_ctx, n_seq, reverse),
        out_shape=jax.ShapeDtypeStruct(shape, jnp.float32),
        in_specs=[vmem],
        out_specs=vmem,
        scratch_shapes=[
            pltpu.VMEM((rounds + 2,) + shape, jnp.float32),
            pltpu.VMEM((max(rounds - 1, 1),) + shape, jnp.float32),
            pltpu.VMEM(shape, jnp.float32),
            pltpu.VMEM(shape, jnp.float32),
            pltpu.VMEM(shape, jnp.float32),
            pltpu.SemaphoreType.DMA((rounds + 2, shape[0])),
            pltpu.SemaphoreType.DMA((rounds + 2, shape[0])),
        ],
        compiler_params=pltpu.CompilerParams(
            collective_id=1 if reverse else 0,
            has_side_effects=True,
            vmem_limit_bytes=48 << 20,
        ),
        name="scan_later" if reverse else "scan_earlier",
    )(x)


def per_device(n_ctx, n_seq, queries, keys, values, grad_output):
    length = queries.shape[0]
    pick_a, pick_b, aux, aux_column = tables()
    whole = pl.BlockSpec((length, LANES), lambda h: (0, 0))
    wide = pl.BlockSpec((length, HEAD_DIM), lambda h: (0, h))
    state = pl.BlockSpec((1, ROWS, HEAD_DIM), lambda h: (h, 0, 0))
    pick = pl.BlockSpec((1, ROWS, LANES), lambda h: (h, 0, 0))
    row = pl.BlockSpec((8, ROWS), lambda h: (0, 0))
    column = pl.BlockSpec((ROWS, LANES), lambda h: (0, 0))
    params = pltpu.CompilerParams(
        dimension_semantics=("arbitrary",), vmem_limit_bytes=48 << 20
    )
    state_shape = jax.ShapeDtypeStruct((HEADS, ROWS, HEAD_DIM), jnp.float32)
    narrow_acc = pltpu.VMEM((length, LANES), jnp.float32)
    f32, bf16 = jnp.float32, jnp.bfloat16

    mine = pl.pallas_call(
        key_state_kernel,
        grid=(HEADS,),
        out_shape=state_shape,
        in_specs=[whole, wide, pick, pick, column],
        out_specs=state,
        compiler_params=params,
        name="key_state",
    )(keys, values, pick_a, pick_b, aux_column)
    prior = scan(mine, n_ctx, n_seq, False)
    attended, grad_query, terms, key_part, value_part = pl.pallas_call(
        middle_kernel,
        grid=(HEADS,),
        out_shape=(
            jax.ShapeDtypeStruct(values.shape, bf16),
            jax.ShapeDtypeStruct(queries.shape, bf16),
            state_shape,
            jax.ShapeDtypeStruct(keys.shape, f32),
            jax.ShapeDtypeStruct(values.shape, f32),
        ),
        in_specs=[whole, whole, wide, wide, state, pick, pick, row, column],
        out_specs=(wide, whole, state, whole, wide),
        scratch_shapes=[narrow_acc, narrow_acc],
        compiler_params=params,
        name="middle",
    )(queries, keys, values, grad_output, prior, pick_a, pick_b, aux, aux_column)
    later = scan(terms, n_ctx, n_seq, True)
    grad_key, grad_value = pl.pallas_call(
        last_kernel,
        grid=(HEADS,),
        out_shape=(
            jax.ShapeDtypeStruct(keys.shape, bf16),
            jax.ShapeDtypeStruct(values.shape, bf16),
        ),
        in_specs=[whole, wide, state, whole, wide, pick, pick, row],
        out_specs=(whole, wide),
        scratch_shapes=[narrow_acc],
        compiler_params=params,
        name="last",
    )(keys, values, later, key_part, value_part, pick_a, pick_b, aux)
    return attended, grad_query, grad_key, grad_value


def solution(mesh):
    placed = P(("seq", "ctx"), None)
    return jax.shard_map(
        functools.partial(per_device, mesh.shape["ctx"], mesh.shape["seq"]),
        mesh=mesh,
        in_specs=(placed,) * 4,
        out_specs=(placed,) * 4,
        check_vma=False,
    )
```

```python
import functools
import math

import jax
import jax.numpy as jnp
import numpy as np
from jax import lax
from jax.experimental import pallas as pl
from jax.experimental.pallas import tpu as pltpu
from jax.sharding import PartitionSpec as P

HEADS = 8
QK_DIM = 16
HEAD_DIM = 128
FEATURES = 153
ROWS = 160
LANES = 128
MESH = pl.DeviceIdType.MESH
NN = (((1,), (0,)), ((), ()))
NT = (((1,), (1,)), ((), ()))
TN = (((0,), (0,)), ((), ()))


def tables():
    upper, lower = np.triu_indices(QK_DIM)
    pick_a = np.zeros((HEADS, ROWS, LANES), np.float32)
    pick_b = np.zeros((HEADS, ROWS, LANES), np.float32)
    aux = np.zeros((8, ROWS), np.float32)
    aux[0, 0] = 1.0
    aux[1, : 1 + QK_DIM] = 1.0
    aux[2, 0] = 1.0
    aux[2, 1 : 1 + QK_DIM] = 1.0 / math.sqrt(math.sqrt(QK_DIM))
    aux[2, 1 + QK_DIM : FEATURES] = np.where(upper == lower, 1.0, math.sqrt(2.0)) / math.sqrt(
        2.0 * QK_DIM
    )
    for head in range(HEADS):
        base = head * QK_DIM
        for i in range(QK_DIM):
            pick_a[head, 1 + i, base + i] = 1.0
        for n, (i, j) in enumerate(zip(upper, lower)):
            pick_a[head, 1 + QK_DIM + n, base + i] = 1.0
            pick_b[head, 1 + QK_DIM + n, base + j] = 1.0
    aux_column = np.zeros((ROWS, LANES), np.float32)
    aux_column[:, :8] = aux.T
    return (
        jnp.asarray(pick_a, jnp.bfloat16),
        jnp.asarray(pick_b, jnp.bfloat16),
        jnp.asarray(aux),
        jnp.asarray(aux_column),
    )


def dot(a, b, dims=NN):
    return lax.dot_general(a, b, dims, preferred_element_type=jnp.float32)


def split(x):
    high = x.astype(jnp.bfloat16)
    return high, (x - high.astype(jnp.float32)).astype(jnp.bfloat16)


def dot2(pair, b, dims=NN):
    return dot(pair[0], b, dims) + dot(pair[1], b, dims)


def dot2r(a, pair, dims=NN):
    return dot(a, pair[0], dims) + dot(a, pair[1], dims)


def dot3(x, y, dims=NN):
    return dot(x[0], y[0], dims) + (dot(x[0], y[1], dims) + dot(x[1], y[0], dims))


def features_by_row(pick_a, pick_b, aux_column, x):
    a = dot(pick_a, x, NT) + aux_column[:, 0:1]
    b = dot(pick_b, x, NT) + aux_column[:, 1:2]
    return a * b * aux_column[:, 2:3]


def factors_by_token(pick_a, pick_b, aux, x):
    a = dot(x, pick_a, NT) + aux[0:1, :]
    b = dot(x, pick_b, NT) + aux[1:2, :]
    return a, b


def put_state(ref, state, norm):
    ref[0] = state
    ref[0, FEATURES : FEATURES + 1, :] = norm[0:1, :LANES]
    ref[0, FEATURES + 1 : FEATURES + 2, : ROWS - LANES] = norm[0:1, LANES:ROWS]


def norm_of(ref):
    return jnp.concatenate(
        [
            ref[0, FEATURES : FEATURES + 1, :],
            ref[0, FEATURES + 1 : FEATURES + 2, : ROWS - LANES],
        ],
        axis=1,
    )


def key_state_kernel(k_ref, v_ref, a_ref, b_ref, auxc_ref, x_ref):
    phi = split(features_by_row(a_ref[0], b_ref[0], auxc_ref, k_ref[...]))
    ones = jnp.ones((8, k_ref.shape[0]), jnp.bfloat16)
    put_state(x_ref, dot2(phi, v_ref[...]), dot2r(ones, phi, NT))


def pull(grad, a, b, pick_a, pick_b):
    return dot2(split(grad * b), pick_a) + dot2(split(grad * a), pick_b)


def middle_kernel(
    q_ref, k_ref, v_ref, g_ref, p_ref, a_ref, b_ref, aux_ref, auxc_ref,
    out_ref, gq_ref, x_ref, gk_ref, gv_ref, gq_acc, gk_acc,
):
    head = pl.program_id(0)
    length = q_ref.shape[0]
    q, k, v, g = q_ref[...], k_ref[...], v_ref[...], g_ref[...]
    pick_a, pick_b = a_ref[0], b_ref[0]
    scale = 1.0 / math.sqrt(QK_DIM)
    mine = lax.broadcasted_iota(jnp.int32, (length, LANES), 1) // QK_DIM == head
    q_mine = jnp.where(mine, q, jnp.zeros_like(q))
    k_mine = jnp.where(mine, k, jnp.zeros_like(k))
    s = dot(q_mine, k, NT) * scale
    causal = lax.broadcasted_iota(jnp.int32, (length, length), 0) >= lax.broadcasted_iota(
        jnp.int32, (length, length), 1
    )
    kern = split(jnp.where(causal, 1.0 + s + 0.5 * s * s, 0.0))
    local = dot2(kern, jnp.concatenate([v, jnp.ones_like(v)], axis=1))
    a, b = factors_by_token(pick_a, pick_b, aux_ref, q)
    phi = a * b * aux_ref[2:3, :]
    prior = split(p_ref[0])
    prior_norm = norm_of(p_ref)
    den = local[:, HEAD_DIM:] + jnp.sum(phi * prior_norm, axis=1, keepdims=True)
    rden = 1.0 / den
    out = (local[:, :HEAD_DIM] + dot3(split(phi), prior)) * rden
    out_ref[...] = out.astype(jnp.bfloat16)
    g32 = g.astype(jnp.float32)
    scaled = split(g32 * rden)
    weighed = g32 * out * rden
    share = jnp.sum(weighed, axis=1, keepdims=True)
    share_row = split(dot2r(jnp.ones((8, LANES), jnp.bfloat16), split(weighed), NT))
    phi_row = split(features_by_row(pick_a, pick_b, auxc_ref, q))
    put_state(x_ref, dot3(phi_row, scaled), dot3(share_row, phi_row, NT))
    rden_column = rden[:, 0:1]
    direct = dot(g, v, NT) * rden_column - share
    grad_dots = split(jnp.where(causal, direct * (1.0 + s) * scale, 0.0))
    gv_ref[...] = dot3(kern, scaled, TN)
    grad_phi = dot2r(g, prior, NT) * rden_column - share * prior_norm
    grad_q = dot2(grad_dots, k_mine) + pull(grad_phi * aux_ref[2:3, :], a, b, pick_a, pick_b)
    grad_k = dot2(grad_dots, q_mine, TN)

    @pl.when(head == 0)
    def _():
        gq_acc[...] = grad_q
        gk_acc[...] = grad_k

    @pl.when(head > 0)
    def _():
        gq_acc[...] += grad_q
        gk_acc[...] += grad_k

    @pl.when(head == HEADS - 1)
    def _():
        gq_ref[...] = gq_acc[...].astype(jnp.bfloat16)
        gk_ref[...] = gk_acc[...]


def last_kernel(
    k_ref, v_ref, l_ref, gk_in, gv_in, a_ref, b_ref, aux_ref, gk_ref, gv_ref, gk_acc
):
    head = pl.program_id(0)
    k, v = k_ref[...], v_ref[...]
    pick_a, pick_b = a_ref[0], b_ref[0]
    later = split(l_ref[0])
    later_norm = norm_of(l_ref)
    a, b = factors_by_token(pick_a, pick_b, aux_ref, k)
    factor = aux_ref[2:3, :]
    gv_ref[...] = (gv_in[...] + dot3(split(a * b * factor), later)).astype(jnp.bfloat16)
    grad_phi = dot2r(v, later, NT) - later_norm
    grad_k = pull(grad_phi * factor, a, b, pick_a, pick_b)

    @pl.when(head == 0)
    def _():
        gk_acc[...] = gk_in[...] + grad_k

    @pl.when(head > 0)
    def _():
        gk_acc[...] += grad_k

    @pl.when(head == HEADS - 1)
    def _():
        gk_ref[...] = gk_acc[...].astype(jnp.bfloat16)


def scan_kernel(
    n_ctx, n_seq, reverse, lags, x_ref, p_ref, peer, other, got, tot, part, before, up_got, up,
    down_got, down, send_sem, recv_sem,
):
    pair_lag, round_lag, share_lag, hop_lag = lags
    rounds = n_seq.bit_length() - 1
    chunks, _, rows, _ = x_ref.shape
    share_at, up_at, down_at = rounds, rounds + 1, rounds + 2
    ctx, seq = lax.axis_index("ctx"), lax.axis_index("seq")
    if reverse:
        place, line = n_ctx - 1 - ctx, n_seq - 1 - seq
        step = -1
    else:
        place, line = ctx, seq
        step = 1
    high = [(line // (1 << r)) % 2 for r in range(rounds)]
    partner = [seq + step * (1 << r) * (1 - 2 * high[r]) for r in range(rounds)]
    mine = high[0]
    theirs = 1 - mine
    has_above = place < n_ctx - 1
    has_below = place > 0
    above = lax.rem(ctx + step + n_ctx, n_ctx)
    below = lax.rem(ctx - step + n_ctx, n_ctx)

    barrier = pltpu.get_barrier_semaphore()
    for r in range(rounds):
        pl.semaphore_signal(barrier, inc=1, device_id=(ctx, partner[r]), device_id_type=MESH)

    @pl.when(has_above)
    def _():
        pl.semaphore_signal(barrier, inc=1, device_id=(above, seq), device_id_type=MESH)

    @pl.when(has_below)
    def _():
        pl.semaphore_signal(barrier, inc=1, device_id=(below, seq), device_id_type=MESH)

    pl.semaphore_wait(
        barrier, rounds + (place + n_ctx - 1) // n_ctx + (n_ctx - 1 - place + n_ctx - 1) // n_ctx
    )

    def copy(stage, c, source, target, device):
        return pltpu.make_async_remote_copy(
            src_ref=source,
            dst_ref=target,
            send_sem=send_sem.at[stage, c],
            recv_sem=recv_sem.at[stage, c],
            device_id=device,
            device_id_type=MESH,
        )

    def swap(c):
        return copy(0, c, x_ref.at[c], peer.at[c], (ctx, partner[0]))

    def exchange(r, c):
        return copy(r, c, tot.at[r - 1, c], got.at[r - 1, c], (ctx, partner[r]))

    def share(c):
        return copy(share_at, c, part.at[c], other.at[c], (ctx, partner[0]))

    def upward(c):
        return copy(up_at, c, up.at[c], up_got.at[c], (above, seq))

    def downward(c):
        return copy(down_at, c, down.at[c], down_got.at[c], (below, seq))

    def first(c):
        swap(c).wait_recv()
        tot[0, c] = x_ref[c, mine] + peer[c, mine]
        exchange(1, c).start()

    def middle(r, c):
        exchange(r, c).wait_recv()
        arrived = got[r - 1, c]
        add = jnp.where(high[r] == 1, arrived, 0.0)
        part[c] = add if r == 1 else part[c] + add
        if r < rounds - 1:
            tot[r, c] = tot[r - 1, c] + arrived
            exchange(r + 1, c).start()
        else:
            share(c).start()

    def joined(c):
        share(c).wait_recv()
        before[c, mine] = part[c] + jnp.where(mine == 1, peer[c, mine], 0.0)
        before[c, theirs] = other[c] + jnp.where(mine == 1, peer[c, theirs], 0.0)

        @pl.when(has_above & ~has_below)
        def _():
            up[c] = before[c] + x_ref[c]
            upward(c).start()

        @pl.when(has_below & ~has_above)
        def _():
            down[c] = before[c]
            downward(c).start()

    def rise(c):
        upward(c).wait_recv()

        @pl.when(has_above)
        def _():
            up[c] = before[c] + x_ref[c] + up_got[c]
            upward(c).start()

    def sink(c):
        downward(c).wait_recv()

        @pl.when(has_below)
        def _():
            down[c] = before[c] + down_got[c]
            downward(c).start()

    for c in range(chunks):
        swap(c).start()

    stages = [(first, pair_lag)]
    at = pair_lag
    for r in range(1, rounds):
        at += round_lag
        stages.append((functools.partial(middle, r), at))
    at += share_lag
    stages.append((joined, at))
    turns = at + hop_lag * (n_ctx - 1) + chunks
    rise_at = at + hop_lag * place
    sink_at = at + hop_lag * (n_ctx - 1 - place)

    def turn(t, _):
        def run(body, start, extra=None):
            c = t - start
            ok = (c >= 0) & (c < chunks)

            @pl.when(ok if extra is None else ok & extra)
            def _():
                body(c)

        run(sink, sink_at, has_above)
        run(rise, rise_at, has_below)
        for body, start in reversed(stages):
            run(body, start)
        return 0

    lax.fori_loop(pair_lag, turns, turn, 0)

    def finish(c, _):
        p_ref[c] = before[c]

        @pl.when(has_below)
        def _():
            p_ref[c] += up_got[c]
            downward(c).wait_send()

        @pl.when(has_above)
        def _():
            p_ref[c] += down_got[c]
            upward(c).wait_send()

        swap(c).wait_send()
        for r in range(1, rounds):
            exchange(r, c).wait_send()
        share(c).wait_send()
        return 0

    lax.fori_loop(0, chunks, finish, 0)


def scan(x, n_ctx, n_seq, reverse, chunks=8, lags=(1, 2, 1, 2)):
    rounds = n_seq.bit_length() - 1
    rows = x.shape[0] * x.shape[1] // (2 * chunks)
    full = (chunks, 2, rows, 128)
    half = (chunks, rows, 128)
    vmem = pl.BlockSpec(memory_space=pltpu.VMEM)
    f32 = jnp.float32
    return pl.pallas_call(
        functools.partial(scan_kernel, n_ctx, n_seq, reverse, lags),
        out_shape=jax.ShapeDtypeStruct(full, f32),
        in_specs=[vmem],
        out_specs=vmem,
        scratch_shapes=[
            pltpu.VMEM(full, f32),
            pltpu.VMEM(half, f32),
            pltpu.VMEM((rounds - 1,) + half, f32),
            pltpu.VMEM((rounds - 1,) + half, f32),
            pltpu.VMEM(half, f32),
            pltpu.VMEM(full, f32),
            pltpu.VMEM(full, f32),
            pltpu.VMEM(full, f32),
            pltpu.VMEM(full, f32),
            pltpu.VMEM(full, f32),
            pltpu.SemaphoreType.DMA((rounds + 3, chunks)),
            pltpu.SemaphoreType.DMA((rounds + 3, chunks)),
        ],
        compiler_params=pltpu.CompilerParams(
            collective_id=1 if reverse else 0,
            has_side_effects=True,
            vmem_limit_bytes=48 << 20,
        ),
        name="scan_later" if reverse else "scan_earlier",
    )(x.reshape(full)).reshape(x.shape)


def per_device(n_ctx, n_seq, queries, keys, values, grad_output):
    length = queries.shape[0]
    pick_a, pick_b, aux, aux_column = tables()
    whole = pl.BlockSpec((length, LANES), lambda h: (0, 0))
    wide = pl.BlockSpec((length, HEAD_DIM), lambda h: (0, h))
    state = pl.BlockSpec((1, ROWS, HEAD_DIM), lambda h: (h, 0, 0))
    pick = pl.BlockSpec((1, ROWS, LANES), lambda h: (h, 0, 0))
    row = pl.BlockSpec((8, ROWS), lambda h: (0, 0))
    column = pl.BlockSpec((ROWS, LANES), lambda h: (0, 0))
    params = pltpu.CompilerParams(
        dimension_semantics=("arbitrary",), vmem_limit_bytes=48 << 20
    )
    state_shape = jax.ShapeDtypeStruct((HEADS, ROWS, HEAD_DIM), jnp.float32)
    narrow_acc = pltpu.VMEM((length, LANES), jnp.float32)
    f32, bf16 = jnp.float32, jnp.bfloat16

    mine = pl.pallas_call(
        key_state_kernel,
        grid=(HEADS,),
        out_shape=state_shape,
        in_specs=[whole, wide, pick, pick, column],
        out_specs=state,
        compiler_params=params,
        name="key_state",
    )(keys, values, pick_a, pick_b, aux_column)
    prior = scan(mine, n_ctx, n_seq, False)
    attended, grad_query, terms, key_part, value_part = pl.pallas_call(
        middle_kernel,
        grid=(HEADS,),
        out_shape=(
            jax.ShapeDtypeStruct(values.shape, bf16),
            jax.ShapeDtypeStruct(queries.shape, bf16),
            state_shape,
            jax.ShapeDtypeStruct(keys.shape, f32),
            jax.ShapeDtypeStruct(values.shape, f32),
        ),
        in_specs=[whole, whole, wide, wide, state, pick, pick, row, column],
        out_specs=(wide, whole, state, whole, wide),
        scratch_shapes=[narrow_acc, narrow_acc],
        compiler_params=params,
        name="middle",
    )(queries, keys, values, grad_output, prior, pick_a, pick_b, aux, aux_column)
    later = scan(terms, n_ctx, n_seq, True)
    grad_key, grad_value = pl.pallas_call(
        last_kernel,
        grid=(HEADS,),
        out_shape=(
            jax.ShapeDtypeStruct(keys.shape, bf16),
            jax.ShapeDtypeStruct(values.shape, bf16),
        ),
        in_specs=[whole, wide, state, whole, wide, pick, pick, row],
        out_specs=(whole, wide),
        scratch_shapes=[narrow_acc],
        compiler_params=params,
        name="last",
    )(keys, values, later, key_part, value_part, pick_a, pick_b, aux)
    return attended, grad_query, grad_key, grad_value


def solution(mesh):
    placed = P(("seq", "ctx"), None)
    return jax.shard_map(
        functools.partial(per_device, mesh.shape["ctx"], mesh.shape["seq"]),
        mesh=mesh,
        in_specs=(placed,) * 4,
        out_specs=(placed,) * 4,
        check_vma=False,
    )
```

```python
import functools
import math

import jax
import jax.numpy as jnp
import numpy as np
from jax import lax
from jax.experimental import pallas as pl
from jax.experimental.pallas import tpu as pltpu
from jax.sharding import PartitionSpec as P

HEADS = 8
QK_DIM = 16
HEAD_DIM = 128
FEATURES = 153
ROWS = 160
LANES = 128
MESH = pl.DeviceIdType.MESH
NN = (((1,), (0,)), ((), ()))
NT = (((1,), (1,)), ((), ()))
TN = (((0,), (0,)), ((), ()))


def tables():
    upper, lower = np.triu_indices(QK_DIM)
    pick_a = np.zeros((HEADS, ROWS, LANES), np.float32)
    pick_b = np.zeros((HEADS, ROWS, LANES), np.float32)
    aux = np.zeros((8, ROWS), np.float32)
    aux[0, 0] = 1.0
    aux[1, : 1 + QK_DIM] = 1.0
    aux[2, 0] = 1.0
    aux[2, 1 : 1 + QK_DIM] = 1.0 / math.sqrt(math.sqrt(QK_DIM))
    aux[2, 1 + QK_DIM : FEATURES] = np.where(upper == lower, 1.0, math.sqrt(2.0)) / math.sqrt(
        2.0 * QK_DIM
    )
    for head in range(HEADS):
        base = head * QK_DIM
        for i in range(QK_DIM):
            pick_a[head, 1 + i, base + i] = 1.0
        for n, (i, j) in enumerate(zip(upper, lower)):
            pick_a[head, 1 + QK_DIM + n, base + i] = 1.0
            pick_b[head, 1 + QK_DIM + n, base + j] = 1.0
    aux_column = np.zeros((ROWS, LANES), np.float32)
    aux_column[:, :8] = aux.T
    return (
        jnp.asarray(pick_a, jnp.bfloat16),
        jnp.asarray(pick_b, jnp.bfloat16),
        jnp.asarray(aux),
        jnp.asarray(aux_column),
    )


def dot(a, b, dims=NN):
    return lax.dot_general(a, b, dims, preferred_element_type=jnp.float32)


def split(x):
    high = x.astype(jnp.bfloat16)
    return high, (x - high.astype(jnp.float32)).astype(jnp.bfloat16)


def dot2(pair, b, dims=NN):
    return dot(pair[0], b, dims) + dot(pair[1], b, dims)


def dot2r(a, pair, dims=NN):
    return dot(a, pair[0], dims) + dot(a, pair[1], dims)


def dot3(x, y, dims=NN):
    return dot(x[0], y[0], dims) + (dot(x[0], y[1], dims) + dot(x[1], y[0], dims))


def features_by_row(pick_a, pick_b, aux_column, x):
    a = dot(pick_a, x, NT) + aux_column[:, 0:1]
    b = dot(pick_b, x, NT) + aux_column[:, 1:2]
    return a * b * aux_column[:, 2:3]


def factors_by_token(pick_a, pick_b, aux, x):
    a = dot(x, pick_a, NT) + aux[0:1, :]
    b = dot(x, pick_b, NT) + aux[1:2, :]
    return a, b


def put_state(ref, head, state, norm):
    ref[head] = state.reshape(2, ROWS // 2, LANES)
    row = FEATURES - ROWS // 2
    ref[head, 1, row : row + 1, :] = norm[0:1, :LANES]
    ref[head, 1, row + 1 : row + 2, : ROWS - LANES] = norm[0:1, LANES:ROWS]


def norm_of(state):
    return jnp.concatenate(
        [state[FEATURES : FEATURES + 1, :], state[FEATURES + 1 : FEATURES + 2, : ROWS - LANES]],
        axis=1,
    )


def pull(grad, a, b, pick_a, pick_b):
    return dot2(split(grad * b), pick_a) + dot2(split(grad * a), pick_b)


class Scan:
    def __init__(self, n_ctx, n_seq, reverse, refs):
        (
            self.x, self.peer, self.other, self.got, self.tot, self.part, self.before,
            self.up_got, self.up, self.down_got, self.down, self.send_sem, self.recv_sem,
        ) = refs
        self.rounds = n_seq.bit_length() - 1
        ctx, seq = lax.axis_index("ctx"), lax.axis_index("seq")
        step = -1 if reverse else 1
        self.n_ctx = n_ctx
        self.place = n_ctx - 1 - ctx if reverse else ctx
        line = n_seq - 1 - seq if reverse else seq
        self.high = [(line // (1 << r)) % 2 for r in range(self.rounds)]
        self.partner = [
            (ctx, seq + step * (1 << r) * (1 - 2 * self.high[r])) for r in range(self.rounds)
        ]
        self.mine = self.high[0]
        self.has_above = self.place < n_ctx - 1
        self.has_below = self.place > 0
        self.above = (lax.rem(ctx + step + n_ctx, n_ctx), seq)
        self.below = (lax.rem(ctx - step + n_ctx, n_ctx), seq)

    def copy(self, stage, c, source, target, device):
        return pltpu.make_async_remote_copy(
            src_ref=source,
            dst_ref=target,
            send_sem=self.send_sem.at[stage, c],
            recv_sem=self.recv_sem.at[stage, c],
            device_id=device,
            device_id_type=MESH,
        )

    def swap(self, c):
        return self.copy(0, c, self.x.at[c], self.peer.at[c], self.partner[0])

    def exchange(self, r, c):
        return self.copy(r, c, self.tot.at[r - 1, c], self.got.at[r - 1, c], self.partner[r])

    def share(self, c):
        return self.copy(
            self.rounds, c, self.part.at[c], self.other.at[c], self.partner[0]
        )

    def upward(self, c):
        return self.copy(self.rounds + 1, c, self.up.at[c], self.up_got.at[c], self.above)

    def downward(self, c):
        return self.copy(self.rounds + 2, c, self.down.at[c], self.down_got.at[c], self.below)

    def first(self, c):
        self.swap(c).wait_recv()
        self.tot[0, c] = self.x[c, self.mine] + self.peer[c, self.mine]
        self.exchange(1, c).start()

    def round(self, r, c):
        self.exchange(r, c).wait_recv()
        arrived = self.got[r - 1, c]
        add = jnp.where(self.high[r] == 1, arrived, 0.0)
        self.part[c] = add if r == 1 else self.part[c] + add
        if r < self.rounds - 1:
            self.tot[r, c] = self.tot[r - 1, c] + arrived
            self.exchange(r + 1, c).start()
        else:
            self.share(c).start()

    def joined(self, c):
        self.share(c).wait_recv()
        mine = self.mine
        for half, value in ((mine, self.part[c]), (1 - mine, self.other[c])):
            self.before[c, half] = value + jnp.where(mine == 1, self.peer[c, half], 0.0)

        @pl.when(self.has_above & ~self.has_below)
        def _():
            self.up[c] = self.before[c] + self.x[c]
            self.upward(c).start()

        @pl.when(self.has_below & ~self.has_above)
        def _():
            self.down[c] = self.before[c]
            self.downward(c).start()

    def rise(self, c):
        self.upward(c).wait_recv()

        @pl.when(self.has_above)
        def _():
            self.up[c] = self.before[c] + self.x[c] + self.up_got[c]
            self.upward(c).start()

    def sink(self, c):
        self.downward(c).wait_recv()

        @pl.when(self.has_below)
        def _():
            self.down[c] = self.before[c] + self.down_got[c]
            self.downward(c).start()

    def result(self, c):
        total = self.before[c]
        total = total + jnp.where(self.has_below, self.up_got[c], 0.0)
        total = total + jnp.where(self.has_above, self.down_got[c], 0.0)
        return total.reshape(ROWS, LANES)

    def stages(self, start, lags):
        pair_lag, round_lag, share_lag, hop_lag = lags
        at = start + pair_lag
        out = [(self.first, at, None)]
        for r in range(1, self.rounds):
            at += round_lag
            out.append((functools.partial(self.round, r), at, None))
        at += share_lag
        out.append((self.joined, at, None))
        out.append((self.rise, at + hop_lag * self.place, self.has_below))
        out.append((self.sink, at + hop_lag * (self.n_ctx - 1 - self.place), self.has_above))
        return out, at + hop_lag * (self.n_ctx - 1)

    def finish(self, c):
        self.swap(c).wait_send()
        for r in range(1, self.rounds):
            self.exchange(r, c).wait_send()
        self.share(c).wait_send()

        @pl.when(self.has_below)
        def _():
            self.downward(c).wait_send()

        @pl.when(self.has_above)
        def _():
            self.upward(c).wait_send()


def kernel(
    n_ctx, n_seq, lags, q_ref, k_ref, v_ref, g_ref, a_ref, b_ref, aux_ref, auxc_ref,
    out_ref, gq_ref, gk_ref, gv_ref, gq_acc, gk_acc, gv_acc, *refs,
):
    count = len(refs) // 2
    earlier = Scan(n_ctx, n_seq, False, refs[:count])
    later = Scan(n_ctx, n_seq, True, refs[count:])
    length = q_ref.shape[0]
    scale = 1.0 / math.sqrt(QK_DIM)

    barrier = pltpu.get_barrier_semaphore()
    for peer in earlier.partner:
        pl.semaphore_signal(barrier, inc=1, device_id=peer, device_id_type=MESH)

    @pl.when(earlier.has_above)
    def _():
        pl.semaphore_signal(barrier, inc=1, device_id=earlier.above, device_id_type=MESH)

    @pl.when(earlier.has_below)
    def _():
        pl.semaphore_signal(barrier, inc=1, device_id=earlier.below, device_id_type=MESH)

    place = earlier.place
    pl.semaphore_wait(
        barrier,
        earlier.rounds + (place + n_ctx - 1) // n_ctx + (n_ctx - 1 - place + n_ctx - 1) // n_ctx,
    )

    gq_acc[...] = jnp.zeros_like(gq_acc)
    gk_acc[...] = jnp.zeros_like(gk_acc)

    def wide(head):
        return pl.ds(pl.multiple_of(head * HEAD_DIM, HEAD_DIM), HEAD_DIM)

    def key_state(head):
        phi = split(features_by_row(a_ref[head], b_ref[head], auxc_ref, k_ref[...]))
        ones = jnp.ones((8, length), jnp.bfloat16)
        put_state(earlier.x, head, dot2(phi, v_ref[:, wide(head)]), dot2r(ones, phi, NT))
        earlier.swap(head).start()

    def middle(head):
        q, k, v, g = q_ref[...], k_ref[...], v_ref[:, wide(head)], g_ref[:, wide(head)]
        pick_a, pick_b = a_ref[head], b_ref[head]
        mine = lax.broadcasted_iota(jnp.int32, (length, LANES), 1) // QK_DIM == head
        q_mine = jnp.where(mine, q, jnp.zeros_like(q))
        k_mine = jnp.where(mine, k, jnp.zeros_like(k))
        s = dot(q_mine, k, NT) * scale
        causal = lax.broadcasted_iota(jnp.int32, (length, length), 0) >= lax.broadcasted_iota(
            jnp.int32, (length, length), 1
        )
        kern = split(jnp.where(causal, 1.0 + s + 0.5 * s * s, 0.0))
        local = dot2(kern, jnp.concatenate([v, jnp.ones_like(v)], axis=1))
        a, b = factors_by_token(pick_a, pick_b, aux_ref, q)
        phi = a * b * aux_ref[2:3, :]
        state = earlier.result(head)
        prior = split(state)
        prior_norm = norm_of(state)
        den = local[:, HEAD_DIM:] + jnp.sum(phi * prior_norm, axis=1, keepdims=True)
        rden = 1.0 / den
        out = (local[:, :HEAD_DIM] + dot3(split(phi), prior)) * rden
        out_ref[:, wide(head)] = out.astype(jnp.bfloat16)
        g32 = g.astype(jnp.float32)
        scaled = split(g32 * rden)
        weighed = g32 * out * rden
        share = jnp.sum(weighed, axis=1, keepdims=True)
        share_row = split(dot2r(jnp.ones((8, LANES), jnp.bfloat16), split(weighed), NT))
        phi_row = split(features_by_row(pick_a, pick_b, auxc_ref, q))
        put_state(later.x, head, dot3(phi_row, scaled), dot3(share_row, phi_row, NT))
        later.swap(head).start()
        rden_column = rden[:, 0:1]
        direct = dot(g, v, NT) * rden_column - share
        grad_dots = split(jnp.where(causal, direct * (1.0 + s) * scale, 0.0))
        gv_acc[:, wide(head)] = dot3(kern, scaled, TN)
        grad_phi = dot2r(g, prior, NT) * rden_column - share * prior_norm
        gq_acc[...] += dot2(grad_dots, k_mine) + pull(
            grad_phi * aux_ref[2:3, :], a, b, pick_a, pick_b
        )
        gk_acc[...] += dot2(grad_dots, q_mine, TN)

    def last(head):
        k, v = k_ref[...], v_ref[:, wide(head)]
        pick_a, pick_b = a_ref[head], b_ref[head]
        state = later.result(head)
        after = split(state)
        a, b = factors_by_token(pick_a, pick_b, aux_ref, k)
        factor = aux_ref[2:3, :]
        grad_v = gv_acc[:, wide(head)] + dot3(split(a * b * factor), after)
        gv_ref[:, wide(head)] = grad_v.astype(jnp.bfloat16)
        grad_phi = dot2r(v, after, NT) - norm_of(state)
        gk_acc[...] += pull(grad_phi * factor, a, b, pick_a, pick_b)

    early_stages, early_done = earlier.stages(0, lags)
    late_stages, late_done = later.stages(early_done, lags)
    plan = list(reversed(late_stages)) + list(reversed(early_stages)) + [
        (key_state, 0, None),
        (middle, early_done, None),
        (last, late_done, None),
    ]

    def turn(t, carry):
        for body, start, condition in plan:
            head = t - start
            ok = (head >= 0) & (head < HEADS)

            @pl.when(ok if condition is None else ok & condition)
            def _(body=body, head=head):
                body(head)

        return carry

    lax.fori_loop(0, late_done + HEADS, turn, 0)
    gq_ref[...] = gq_acc[...].astype(jnp.bfloat16)
    gk_ref[...] = gk_acc[...].astype(jnp.bfloat16)

    def finish(c, carry):
        earlier.finish(c)
        later.finish(c)
        return carry

    lax.fori_loop(0, HEADS, finish, 0)


def per_device(n_ctx, n_seq, queries, keys, values, grad_output):
    length = queries.shape[0]
    rounds = n_seq.bit_length() - 1
    f32, bf16 = jnp.float32, jnp.bfloat16
    full = pltpu.VMEM((HEADS, 2, ROWS // 2, LANES), f32)
    half = pltpu.VMEM((HEADS, ROWS // 2, LANES), f32)
    halves = pltpu.VMEM((rounds - 1, HEADS, ROWS // 2, LANES), f32)
    semaphores = pltpu.SemaphoreType.DMA((rounds + 3, HEADS))
    scan = [full, full, half, halves, halves, half, full, full, full, full, full]
    scan += [semaphores, semaphores]
    narrow = pltpu.VMEM((length, LANES), f32)
    vmem = pl.BlockSpec(memory_space=pltpu.VMEM)
    return pl.pallas_call(
        functools.partial(kernel, n_ctx, n_seq, (1, 2, 1, 2)),
        out_shape=(
            jax.ShapeDtypeStruct(values.shape, bf16),
            jax.ShapeDtypeStruct(queries.shape, bf16),
            jax.ShapeDtypeStruct(keys.shape, bf16),
            jax.ShapeDtypeStruct(values.shape, bf16),
        ),
        in_specs=[vmem] * 8,
        out_specs=(vmem,) * 4,
        scratch_shapes=[narrow, narrow, pltpu.VMEM(values.shape, f32)] + scan + scan,
        compiler_params=pltpu.CompilerParams(
            collective_id=0, has_side_effects=True, vmem_limit_bytes=56 << 20
        ),
        name="attention",
    )(queries, keys, values, grad_output, *tables())


def solution(mesh):
    placed = P(("seq", "ctx"), None)
    return jax.shard_map(
        functools.partial(per_device, mesh.shape["ctx"], mesh.shape["seq"]),
        mesh=mesh,
        in_specs=(placed,) * 4,
        out_specs=(placed,) * 4,
        check_vma=False,
    )
```

```python
import functools
import math

import jax
import jax.numpy as jnp
import numpy as np
from jax import lax
from jax.experimental import pallas as pl
from jax.experimental.pallas import tpu as pltpu
from jax.sharding import PartitionSpec as P

HEADS = 8
QK_DIM = 16
HEAD_DIM = 128
FEATURES = 153
ROWS = 160
LANES = 128
MESH = pl.DeviceIdType.MESH
NN = (((1,), (0,)), ((), ()))
NT = (((1,), (1,)), ((), ()))
TN = (((0,), (0,)), ((), ()))


def tables():
    upper, lower = np.triu_indices(QK_DIM)
    pick_a = np.zeros((HEADS, ROWS, LANES), np.float32)
    pick_b = np.zeros((HEADS, ROWS, LANES), np.float32)
    aux = np.zeros((8, ROWS), np.float32)
    aux[0, 0] = 1.0
    aux[1, : 1 + QK_DIM] = 1.0
    aux[2, 0] = 1.0
    aux[2, 1 : 1 + QK_DIM] = 1.0 / math.sqrt(math.sqrt(QK_DIM))
    aux[2, 1 + QK_DIM : FEATURES] = np.where(upper == lower, 1.0, math.sqrt(2.0)) / math.sqrt(
        2.0 * QK_DIM
    )
    for head in range(HEADS):
        base = head * QK_DIM
        for i in range(QK_DIM):
            pick_a[head, 1 + i, base + i] = 1.0
        for n, (i, j) in enumerate(zip(upper, lower)):
            pick_a[head, 1 + QK_DIM + n, base + i] = 1.0
            pick_b[head, 1 + QK_DIM + n, base + j] = 1.0
    aux_column = np.zeros((ROWS, LANES), np.float32)
    aux_column[:, :8] = aux.T
    return (
        jnp.asarray(pick_a, jnp.bfloat16),
        jnp.asarray(pick_b, jnp.bfloat16),
        jnp.asarray(aux),
        jnp.asarray(aux_column),
    )


def dot(a, b, dims=NN):
    return lax.dot_general(a, b, dims, preferred_element_type=jnp.float32)


def split(x):
    high = x.astype(jnp.bfloat16)
    return high, (x - high.astype(jnp.float32)).astype(jnp.bfloat16)


def dot2(pair, b, dims=NN):
    return dot(pair[0], b, dims) + dot(pair[1], b, dims)


def dot2r(a, pair, dims=NN):
    return dot(a, pair[0], dims) + dot(a, pair[1], dims)


def dot3(x, y, dims=NN):
    return dot(x[0], y[0], dims) + (dot(x[0], y[1], dims) + dot(x[1], y[0], dims))


def features_by_row(pick_a, pick_b, aux_column, x):
    a = dot(pick_a, x, NT) + aux_column[:, 0:1]
    b = dot(pick_b, x, NT) + aux_column[:, 1:2]
    return a * b * aux_column[:, 2:3]


def factors_by_token(pick_a, pick_b, aux, x):
    a = dot(x, pick_a, NT) + aux[0:1, :]
    b = dot(x, pick_b, NT) + aux[1:2, :]
    return a, b


def put_state(ref, head, state, norm):
    ref[head] = state.reshape(2, ROWS // 2, LANES)
    row = FEATURES - ROWS // 2
    ref[head, 1, row : row + 1, :] = norm[0:1, :LANES]
    ref[head, 1, row + 1 : row + 2, : ROWS - LANES] = norm[0:1, LANES:ROWS]


def norm_of(state):
    return jnp.concatenate(
        [state[FEATURES : FEATURES + 1, :], state[FEATURES + 1 : FEATURES + 2, : ROWS - LANES]],
        axis=1,
    )


def pull(grad, a, b, pick_a, pick_b):
    return dot2(split(grad * b), pick_a) + dot2(split(grad * a), pick_b)


class Scan:
    def __init__(self, n_ctx, n_seq, reverse, refs):
        (
            self.x, self.peer, self.other, self.got, self.tot, self.part, self.before,
            self.up_got, self.up, self.down_got, self.down, self.send_sem, self.recv_sem,
        ) = refs
        self.rounds = n_seq.bit_length() - 1
        ctx, seq = lax.axis_index("ctx"), lax.axis_index("seq")
        step = -1 if reverse else 1
        self.n_ctx = n_ctx
        self.place = n_ctx - 1 - ctx if reverse else ctx
        line = n_seq - 1 - seq if reverse else seq
        self.high = [(line // (1 << r)) % 2 for r in range(self.rounds)]
        self.partner = [
            (ctx, seq + step * (1 << r) * (1 - 2 * self.high[r])) for r in range(self.rounds)
        ]
        self.mine = self.high[0]
        self.has_above = self.place < n_ctx - 1
        self.has_below = self.place > 0
        self.above = (lax.rem(ctx + step + n_ctx, n_ctx), seq)
        self.below = (lax.rem(ctx - step + n_ctx, n_ctx), seq)

    def copy(self, stage, c, source, target, device):
        return pltpu.make_async_remote_copy(
            src_ref=source,
            dst_ref=target,
            send_sem=self.send_sem.at[stage, c],
            recv_sem=self.recv_sem.at[stage, c],
            device_id=device,
            device_id_type=MESH,
        )

    def swap(self, c):
        return self.copy(0, c, self.x.at[c], self.peer.at[c], self.partner[0])

    def exchange(self, r, c):
        return self.copy(r, c, self.tot.at[r - 1, c], self.got.at[r - 1, c], self.partner[r])

    def share(self, c):
        return self.copy(
            self.rounds, c, self.part.at[c], self.other.at[c], self.partner[0]
        )

    def upward(self, c):
        return self.copy(self.rounds + 1, c, self.up.at[c], self.up_got.at[c], self.above)

    def downward(self, c):
        return self.copy(self.rounds + 2, c, self.down.at[c], self.down_got.at[c], self.below)

    def first(self, c):
        self.swap(c).wait_recv()
        self.tot[0, c] = self.x[c, self.mine] + self.peer[c, self.mine]
        self.exchange(1, c).start()

    def round(self, r, c):
        self.exchange(r, c).wait_recv()
        arrived = self.got[r - 1, c]
        add = jnp.where(self.high[r] == 1, arrived, 0.0)
        self.part[c] = add if r == 1 else self.part[c] + add
        if r < self.rounds - 1:
            self.tot[r, c] = self.tot[r - 1, c] + arrived
            self.exchange(r + 1, c).start()
        else:
            self.share(c).start()

    def joined(self, c):
        self.share(c).wait_recv()
        mine = self.mine
        for half, value in ((mine, self.part[c]), (1 - mine, self.other[c])):
            self.before[c, half] = value + jnp.where(mine == 1, self.peer[c, half], 0.0)

        @pl.when(self.has_above & ~self.has_below)
        def _():
            self.up[c] = self.before[c] + self.x[c]
            self.upward(c).start()

        @pl.when(self.has_below & ~self.has_above)
        def _():
            self.down[c] = self.before[c]
            self.downward(c).start()

    def rise(self, c):
        self.upward(c).wait_recv()

        @pl.when(self.has_above)
        def _():
            self.up[c] = self.before[c] + self.x[c] + self.up_got[c]
            self.upward(c).start()

    def sink(self, c):
        self.downward(c).wait_recv()

        @pl.when(self.has_below)
        def _():
            self.down[c] = self.before[c] + self.down_got[c]
            self.downward(c).start()

    def result(self, c):
        total = self.before[c]
        total = total + jnp.where(self.has_below, self.up_got[c], 0.0)
        total = total + jnp.where(self.has_above, self.down_got[c], 0.0)
        return total.reshape(ROWS, LANES)

    def stages(self, start, lags):
        pair_lag, round_lag, share_lag, hop_lag = lags
        at = start + pair_lag
        out = [(self.first, at, None)]
        for r in range(1, self.rounds):
            at += round_lag
            out.append((functools.partial(self.round, r), at, None))
        at += share_lag
        out.append((self.joined, at, None))
        out.append((self.rise, at + hop_lag * self.place, self.has_below))
        out.append((self.sink, at + hop_lag * (self.n_ctx - 1 - self.place), self.has_above))
        return out, at + hop_lag * (self.n_ctx - 1)

    def finish(self, c):
        self.swap(c).wait_send()
        for r in range(1, self.rounds):
            self.exchange(r, c).wait_send()
        self.share(c).wait_send()

        @pl.when(self.has_below)
        def _():
            self.downward(c).wait_send()

        @pl.when(self.has_above)
        def _():
            self.upward(c).wait_send()


def kernel(
    n_ctx, n_seq, lags, q_ref, k_ref, v_ref, g_ref, a_ref, b_ref, aux_ref, auxc_ref,
    out_ref, gq_ref, gk_ref, gv_ref, gq_acc, gk_acc, gv_acc, *refs,
):
    count = len(refs) // 2
    earlier = Scan(n_ctx, n_seq, False, refs[:count])
    later = Scan(n_ctx, n_seq, True, refs[count:])
    length = q_ref.shape[0]
    scale = 1.0 / math.sqrt(QK_DIM)

    barrier = pltpu.get_barrier_semaphore()
    for peer in earlier.partner:
        pl.semaphore_signal(barrier, inc=1, device_id=peer, device_id_type=MESH)

    @pl.when(earlier.has_above)
    def _():
        pl.semaphore_signal(barrier, inc=1, device_id=earlier.above, device_id_type=MESH)

    @pl.when(earlier.has_below)
    def _():
        pl.semaphore_signal(barrier, inc=1, device_id=earlier.below, device_id_type=MESH)

    place = earlier.place
    pl.semaphore_wait(
        barrier,
        earlier.rounds + (place + n_ctx - 1) // n_ctx + (n_ctx - 1 - place + n_ctx - 1) // n_ctx,
    )

    gq_acc[...] = jnp.zeros_like(gq_acc)
    gk_acc[...] = jnp.zeros_like(gk_acc)

    def wide(head):
        return pl.ds(pl.multiple_of(head * HEAD_DIM, HEAD_DIM), HEAD_DIM)

    def key_state(head):
        phi = split(features_by_row(a_ref[head], b_ref[head], auxc_ref, k_ref[...]))
        ones = jnp.ones((8, length), jnp.bfloat16)
        put_state(earlier.x, head, dot2(phi, v_ref[:, wide(head)]), dot2r(ones, phi, NT))
        earlier.swap(head).start()

    def middle(head):
        q, k, v, g = q_ref[...], k_ref[...], v_ref[:, wide(head)], g_ref[:, wide(head)]
        pick_a, pick_b = a_ref[head], b_ref[head]
        mine = lax.broadcasted_iota(jnp.int32, (length, LANES), 1) // QK_DIM == head
        q_mine = jnp.where(mine, q, jnp.zeros_like(q))
        k_mine = jnp.where(mine, k, jnp.zeros_like(k))
        s = dot(q_mine, k, NT) * scale
        causal = lax.broadcasted_iota(jnp.int32, (length, length), 0) >= lax.broadcasted_iota(
            jnp.int32, (length, length), 1
        )
        kern = split(jnp.where(causal, 1.0 + s + 0.5 * s * s, 0.0))
        local = dot2(kern, jnp.concatenate([v, jnp.ones_like(v)], axis=1))
        a, b = factors_by_token(pick_a, pick_b, aux_ref, q)
        phi = a * b * aux_ref[2:3, :]
        state = earlier.result(head)
        prior = split(state)
        prior_norm = norm_of(state)
        den = local[:, HEAD_DIM:] + jnp.sum(phi * prior_norm, axis=1, keepdims=True)
        rden = 1.0 / den
        out = (local[:, :HEAD_DIM] + dot3(split(phi), prior)) * rden
        out_ref[:, wide(head)] = out.astype(jnp.bfloat16)
        g32 = g.astype(jnp.float32)
        scaled = split(g32 * rden)
        weighed = g32 * out * rden
        share = jnp.sum(weighed, axis=1, keepdims=True)
        share_row = split(dot2r(jnp.ones((8, LANES), jnp.bfloat16), split(weighed), NT))
        phi_row = split(features_by_row(pick_a, pick_b, auxc_ref, q))
        put_state(later.x, head, dot3(phi_row, scaled), dot3(share_row, phi_row, NT))
        later.swap(head).start()
        rden_column = rden[:, 0:1]
        direct = dot(g, v, NT) * rden_column - share
        grad_dots = split(jnp.where(causal, direct * (1.0 + s) * scale, 0.0))
        gv_acc[:, wide(head)] = dot3(kern, scaled, TN)
        grad_phi = dot2r(g, prior, NT) * rden_column - share * prior_norm
        gq_acc[...] += dot2(grad_dots, k_mine) + pull(
            grad_phi * aux_ref[2:3, :], a, b, pick_a, pick_b
        )
        gk_acc[...] += dot2(grad_dots, q_mine, TN)

    def last(head):
        k, v = k_ref[...], v_ref[:, wide(head)]
        pick_a, pick_b = a_ref[head], b_ref[head]
        state = later.result(head)
        after = split(state)
        a, b = factors_by_token(pick_a, pick_b, aux_ref, k)
        factor = aux_ref[2:3, :]
        grad_v = gv_acc[:, wide(head)] + dot3(split(a * b * factor), after)
        gv_ref[:, wide(head)] = grad_v.astype(jnp.bfloat16)
        grad_phi = dot2r(v, after, NT) - norm_of(state)
        gk_acc[...] += pull(grad_phi * factor, a, b, pick_a, pick_b)

    early_stages, early_done = earlier.stages(0, lags)
    late_stages, late_done = later.stages(early_done, lags)
    plan = list(reversed(late_stages)) + list(reversed(early_stages)) + [
        (key_state, 0, None),
        (middle, early_done, None),
        (last, late_done, None),
    ]

    def turn(t, carry):
        for body, start, condition in plan:
            head = t - start
            ok = (head >= 0) & (head < HEADS)

            @pl.when(ok if condition is None else ok & condition)
            def _(body=body, head=head):
                body(head)

        return carry

    lax.fori_loop(0, late_done + HEADS, turn, 0)
    gq_ref[...] = gq_acc[...].astype(jnp.bfloat16)
    gk_ref[...] = gk_acc[...].astype(jnp.bfloat16)

    def finish(c, carry):
        earlier.finish(c)
        later.finish(c)
        return carry

    lax.fori_loop(0, HEADS, finish, 0)


def deliver(*refs):
    sem = refs[8]
    copies = [pltpu.make_async_copy(refs[i], refs[4 + i], sem.at[i]) for i in range(4)]
    for copy in copies:
        copy.start()
    for copy in copies:
        copy.wait()


def per_device(n_ctx, n_seq, queries, keys, values, grad_output):
    length = queries.shape[0]
    rounds = n_seq.bit_length() - 1
    f32, bf16 = jnp.float32, jnp.bfloat16
    full = pltpu.VMEM((HEADS, 2, ROWS // 2, LANES), f32)
    half = pltpu.VMEM((HEADS, ROWS // 2, LANES), f32)
    halves = pltpu.VMEM((rounds - 1, HEADS, ROWS // 2, LANES), f32)
    semaphores = pltpu.SemaphoreType.DMA((rounds + 3, HEADS))
    scan = [full, full, half, halves, halves, half, full, full, full, full, full]
    scan += [semaphores, semaphores]
    narrow = pltpu.VMEM((length, LANES), f32)
    vmem = pl.BlockSpec(memory_space=pltpu.VMEM)
    results = pl.pallas_call(
        functools.partial(kernel, n_ctx, n_seq, (1, 2, 1, 2)),
        out_shape=(
            jax.ShapeDtypeStruct(values.shape, bf16),
            jax.ShapeDtypeStruct(queries.shape, bf16),
            jax.ShapeDtypeStruct(keys.shape, bf16),
            jax.ShapeDtypeStruct(values.shape, bf16),
        ),
        in_specs=[vmem] * 8,
        out_specs=(vmem,) * 4,
        scratch_shapes=[narrow, narrow, pltpu.VMEM(values.shape, f32)] + scan + scan,
        compiler_params=pltpu.CompilerParams(
            collective_id=0, has_side_effects=True, vmem_limit_bytes=56 << 20
        ),
        name="attention",
    )(queries, keys, values, grad_output, *tables())
    anywhere = pl.BlockSpec(memory_space=pl.ANY)
    inside = pl.BlockSpec(memory_space=pltpu.VMEM)
    return pl.pallas_call(
        deliver,
        out_shape=tuple(jax.ShapeDtypeStruct(a.shape, a.dtype) for a in results),
        in_specs=[inside] * 4,
        out_specs=(anywhere,) * 4,
        scratch_shapes=[pltpu.SemaphoreType.DMA((4,))],
        name="deliver",
    )(*results)


def solution(mesh):
    placed = P(("seq", "ctx"), None)
    return jax.shard_map(
        functools.partial(per_device, mesh.shape["ctx"], mesh.shape["seq"]),
        mesh=mesh,
        in_specs=(placed,) * 4,
        out_specs=(placed,) * 4,
        check_vma=False,
    )
```

```python
import functools
import math

import jax
import jax.numpy as jnp
import numpy as np
from jax import lax
from jax.experimental import pallas as pl
from jax.experimental.pallas import tpu as pltpu
from jax.sharding import PartitionSpec as P

HEADS = 8
QK_DIM = 16
HEAD_DIM = 128
FEATURES = 153
ROWS = 160
LANES = 128
MESH = pl.DeviceIdType.MESH
NN = (((1,), (0,)), ((), ()))
NT = (((1,), (1,)), ((), ()))
TN = (((0,), (0,)), ((), ()))


def tables():
    upper, lower = np.triu_indices(QK_DIM)
    pick_a = np.zeros((HEADS, ROWS, LANES), np.float32)
    pick_b = np.zeros((HEADS, ROWS, LANES), np.float32)
    aux = np.zeros((8, ROWS), np.float32)
    aux[0, 0] = 1.0
    aux[1, : 1 + QK_DIM] = 1.0
    aux[2, 0] = 1.0
    aux[2, 1 : 1 + QK_DIM] = 1.0 / math.sqrt(math.sqrt(QK_DIM))
    aux[2, 1 + QK_DIM : FEATURES] = np.where(upper == lower, 1.0, math.sqrt(2.0)) / math.sqrt(
        2.0 * QK_DIM
    )
    for head in range(HEADS):
        base = head * QK_DIM
        for i in range(QK_DIM):
            pick_a[head, 1 + i, base + i] = 1.0
        for n, (i, j) in enumerate(zip(upper, lower)):
            pick_a[head, 1 + QK_DIM + n, base + i] = 1.0
            pick_b[head, 1 + QK_DIM + n, base + j] = 1.0
    aux_column = np.zeros((ROWS, LANES), np.float32)
    aux_column[:, :8] = aux.T
    return (
        jnp.asarray(pick_a, jnp.bfloat16),
        jnp.asarray(pick_b, jnp.bfloat16),
        jnp.asarray(aux),
        jnp.asarray(aux_column),
    )


def dot(a, b, dims=NN):
    return lax.dot_general(a, b, dims, preferred_element_type=jnp.float32)


def split(x):
    high = x.astype(jnp.bfloat16)
    return high, (x - high.astype(jnp.float32)).astype(jnp.bfloat16)


def dot2(pair, b, dims=NN):
    return dot(pair[0], b, dims) + dot(pair[1], b, dims)


def dot2r(a, pair, dims=NN):
    return dot(a, pair[0], dims) + dot(a, pair[1], dims)


def dot3(x, y, dims=NN):
    return dot(x[0], y[0], dims) + (dot(x[0], y[1], dims) + dot(x[1], y[0], dims))


def features_by_row(pick_a, pick_b, aux_column, x):
    a = dot(pick_a, x, NT) + aux_column[:, 0:1]
    b = dot(pick_b, x, NT) + aux_column[:, 1:2]
    return a * b * aux_column[:, 2:3]


def factors_by_token(pick_a, pick_b, aux, x):
    a = dot(x, pick_a, NT) + aux[0:1, :]
    b = dot(x, pick_b, NT) + aux[1:2, :]
    return a, b


def put_state(ref, head, state, norm):
    ref[head] = state.reshape(2, ROWS // 2, LANES)
    row = FEATURES - ROWS // 2
    ref[head, 1, row : row + 1, :] = norm[0:1, :LANES]
    ref[head, 1, row + 1 : row + 2, : ROWS - LANES] = norm[0:1, LANES:ROWS]


def norm_of(state):
    return jnp.concatenate(
        [state[FEATURES : FEATURES + 1, :], state[FEATURES + 1 : FEATURES + 2, : ROWS - LANES]],
        axis=1,
    )


def pull(grad, a, b, pick_a, pick_b):
    return dot2(split(grad * b), pick_a) + dot2(split(grad * a), pick_b)


class Scan:
    def __init__(self, n_ctx, n_seq, reverse, refs):
        (
            self.x, self.peer, self.other, self.got, self.tot, self.part, self.before,
            self.up_got, self.up, self.down_got, self.down, self.send_sem, self.recv_sem,
        ) = refs
        self.rounds = n_seq.bit_length() - 1
        ctx, seq = lax.axis_index("ctx"), lax.axis_index("seq")
        step = -1 if reverse else 1
        self.n_ctx = n_ctx
        self.place = n_ctx - 1 - ctx if reverse else ctx
        line = n_seq - 1 - seq if reverse else seq
        self.high = [(line // (1 << r)) % 2 for r in range(self.rounds)]
        self.partner = [
            (ctx, seq + step * (1 << r) * (1 - 2 * self.high[r])) for r in range(self.rounds)
        ]
        self.mine = self.high[0]
        self.has_above = self.place < n_ctx - 1
        self.has_below = self.place > 0
        self.above = (lax.rem(ctx + step + n_ctx, n_ctx), seq)
        self.below = (lax.rem(ctx - step + n_ctx, n_ctx), seq)

    def copy(self, stage, c, source, target, device):
        return pltpu.make_async_remote_copy(
            src_ref=source,
            dst_ref=target,
            send_sem=self.send_sem.at[stage, c],
            recv_sem=self.recv_sem.at[stage, c],
            device_id=device,
            device_id_type=MESH,
        )

    def swap(self, c):
        return self.copy(0, c, self.x.at[c], self.peer.at[c], self.partner[0])

    def exchange(self, r, c):
        return self.copy(r, c, self.tot.at[r - 1, c], self.got.at[r - 1, c], self.partner[r])

    def share(self, c):
        return self.copy(
            self.rounds, c, self.part.at[c], self.other.at[c], self.partner[0]
        )

    def upward(self, c):
        return self.copy(self.rounds + 1, c, self.up.at[c], self.up_got.at[c], self.above)

    def downward(self, c):
        return self.copy(self.rounds + 2, c, self.down.at[c], self.down_got.at[c], self.below)

    def first(self, c):
        self.swap(c).wait_recv()
        self.tot[0, c] = self.x[c, self.mine] + self.peer[c, self.mine]
        self.exchange(1, c).start()

    def round(self, r, c):
        self.exchange(r, c).wait_recv()
        arrived = self.got[r - 1, c]
        add = jnp.where(self.high[r] == 1, arrived, 0.0)
        self.part[c] = add if r == 1 else self.part[c] + add
        if r < self.rounds - 1:
            self.tot[r, c] = self.tot[r - 1, c] + arrived
            self.exchange(r + 1, c).start()
        else:
            self.share(c).start()

    def joined(self, c):
        self.share(c).wait_recv()
        mine = self.mine
        for half, value in ((mine, self.part[c]), (1 - mine, self.other[c])):
            self.before[c, half] = value + jnp.where(mine == 1, self.peer[c, half], 0.0)

        @pl.when(self.has_above & ~self.has_below)
        def _():
            self.up[c] = self.before[c] + self.x[c]
            self.upward(c).start()

        @pl.when(self.has_below & ~self.has_above)
        def _():
            self.down[c] = self.before[c]
            self.downward(c).start()

    def rise(self, c):
        self.upward(c).wait_recv()

        @pl.when(self.has_above)
        def _():
            self.up[c] = self.before[c] + self.x[c] + self.up_got[c]
            self.upward(c).start()

    def sink(self, c):
        self.downward(c).wait_recv()

        @pl.when(self.has_below)
        def _():
            self.down[c] = self.before[c] + self.down_got[c]
            self.downward(c).start()

    def result(self, c):
        total = self.before[c]
        total = total + jnp.where(self.has_below, self.up_got[c], 0.0)
        total = total + jnp.where(self.has_above, self.down_got[c], 0.0)
        return total.reshape(ROWS, LANES)

    def stages(self, start, lags):
        pair_lag, round_lag, share_lag, hop_lag = lags
        at = start + pair_lag
        out = [(self.first, at, None)]
        for r in range(1, self.rounds):
            at += round_lag
            out.append((functools.partial(self.round, r), at, None))
        at += share_lag
        out.append((self.joined, at, None))
        out.append((self.rise, at + hop_lag * self.place, self.has_below))
        out.append((self.sink, at + hop_lag * (self.n_ctx - 1 - self.place), self.has_above))
        return out, at + hop_lag * (self.n_ctx - 1)

    def finish(self, c):
        self.swap(c).wait_send()
        for r in range(1, self.rounds):
            self.exchange(r, c).wait_send()
        self.share(c).wait_send()

        @pl.when(self.has_below)
        def _():
            self.downward(c).wait_send()

        @pl.when(self.has_above)
        def _():
            self.upward(c).wait_send()


def kernel(
    n_ctx, n_seq, lags, q_ref, k_ref, v_ref, g_ref, a_ref, b_ref, aux_ref, auxc_ref,
    out_ref, gq_ref, gk_ref, gv_ref, gq_acc, gk_acc, gv_acc, rden_kept, share_kept, local_kept, *refs,
):
    count = len(refs) // 2
    earlier = Scan(n_ctx, n_seq, False, refs[:count])
    later = Scan(n_ctx, n_seq, True, refs[count:])
    length = q_ref.shape[0]
    scale = 1.0 / math.sqrt(QK_DIM)

    barrier = pltpu.get_barrier_semaphore()
    for peer in earlier.partner:
        pl.semaphore_signal(barrier, inc=1, device_id=peer, device_id_type=MESH)

    @pl.when(earlier.has_above)
    def _():
        pl.semaphore_signal(barrier, inc=1, device_id=earlier.above, device_id_type=MESH)

    @pl.when(earlier.has_below)
    def _():
        pl.semaphore_signal(barrier, inc=1, device_id=earlier.below, device_id_type=MESH)

    place = earlier.place
    pl.semaphore_wait(
        barrier,
        earlier.rounds + (place + n_ctx - 1) // n_ctx + (n_ctx - 1 - place + n_ctx - 1) // n_ctx,
    )

    gq_acc[...] = jnp.zeros_like(gq_acc)
    gk_acc[...] = jnp.zeros_like(gk_acc)

    def wide(head):
        return pl.ds(pl.multiple_of(head * HEAD_DIM, HEAD_DIM), HEAD_DIM)

    def key_state(head):
        phi = split(features_by_row(a_ref[head], b_ref[head], auxc_ref, k_ref[...]))
        ones = jnp.ones((8, length), jnp.bfloat16)
        put_state(earlier.x, head, dot2(phi, v_ref[:, wide(head)]), dot2r(ones, phi, NT))
        earlier.swap(head).start()

    def prepare(head):
        q, k, v = q_ref[...], k_ref[...], v_ref[:, wide(head)]
        mine = lax.broadcasted_iota(jnp.int32, (length, LANES), 1) // QK_DIM == head
        q_mine = jnp.where(mine, q, jnp.zeros_like(q))
        s = dot(q_mine, k, NT) * scale
        causal = lax.broadcasted_iota(jnp.int32, (length, length), 0) >= lax.broadcasted_iota(
            jnp.int32, (length, length), 1
        )
        kern = split(jnp.where(causal, 1.0 + s + 0.5 * s * s, 0.0))
        local_kept[head] = dot2(kern, jnp.concatenate([v, jnp.ones_like(v)], axis=1))

    def middle(head):
        q, g = q_ref[...], g_ref[:, wide(head)]
        pick_a, pick_b = a_ref[head], b_ref[head]
        local = local_kept[head]
        a, b = factors_by_token(pick_a, pick_b, aux_ref, q)
        phi = a * b * aux_ref[2:3, :]
        state = earlier.result(head)
        prior = split(state)
        prior_norm = norm_of(state)
        den = local[:, HEAD_DIM:] + jnp.sum(phi * prior_norm, axis=1, keepdims=True)
        rden = 1.0 / den
        out = (local[:, :HEAD_DIM] + dot3(split(phi), prior)) * rden
        out_ref[:, wide(head)] = out.astype(jnp.bfloat16)
        g32 = g.astype(jnp.float32)
        scaled = split(g32 * rden)
        weighed = g32 * out * rden
        share = jnp.sum(weighed, axis=1, keepdims=True)
        share_row = split(dot2r(jnp.ones((8, LANES), jnp.bfloat16), split(weighed), NT))
        phi_row = split(features_by_row(pick_a, pick_b, auxc_ref, q))
        put_state(later.x, head, dot3(phi_row, scaled), dot3(share_row, phi_row, NT))
        later.swap(head).start()
        rden_kept[head] = rden
        share_kept[head] = jnp.broadcast_to(share, rden.shape)

    def local_gradients(head):
        q, k, v, g = q_ref[...], k_ref[...], v_ref[:, wide(head)], g_ref[:, wide(head)]
        pick_a, pick_b = a_ref[head], b_ref[head]
        mine = lax.broadcasted_iota(jnp.int32, (length, LANES), 1) // QK_DIM == head
        q_mine = jnp.where(mine, q, jnp.zeros_like(q))
        k_mine = jnp.where(mine, k, jnp.zeros_like(k))
        s = dot(q_mine, k, NT) * scale
        causal = lax.broadcasted_iota(jnp.int32, (length, length), 0) >= lax.broadcasted_iota(
            jnp.int32, (length, length), 1
        )
        kern = split(jnp.where(causal, 1.0 + s + 0.5 * s * s, 0.0))
        a, b = factors_by_token(pick_a, pick_b, aux_ref, q)
        state = earlier.result(head)
        prior = split(state)
        prior_norm = norm_of(state)
        rden = rden_kept[head]
        share = share_kept[head][:, 0:1]
        scaled = split(g.astype(jnp.float32) * rden)
        rden_column = rden[:, 0:1]
        direct = dot(g, v, NT) * rden_column - share
        grad_dots = split(jnp.where(causal, direct * (1.0 + s) * scale, 0.0))
        gv_acc[:, wide(head)] = dot3(kern, scaled, TN)
        grad_phi = dot2r(g, prior, NT) * rden_column - share * prior_norm
        gq_acc[...] += dot2(grad_dots, k_mine) + pull(
            grad_phi * aux_ref[2:3, :], a, b, pick_a, pick_b
        )
        gk_acc[...] += dot2(grad_dots, q_mine, TN)

    def last(head):
        k, v = k_ref[...], v_ref[:, wide(head)]
        pick_a, pick_b = a_ref[head], b_ref[head]
        state = later.result(head)
        after = split(state)
        a, b = factors_by_token(pick_a, pick_b, aux_ref, k)
        factor = aux_ref[2:3, :]
        grad_v = gv_acc[:, wide(head)] + dot3(split(a * b * factor), after)
        gv_ref[:, wide(head)] = grad_v.astype(jnp.bfloat16)
        grad_phi = dot2r(v, after, NT) - norm_of(state)
        gk_acc[...] += pull(grad_phi * factor, a, b, pick_a, pick_b)

    early_stages, early_done = earlier.stages(0, lags)
    late_stages, late_done = later.stages(early_done, lags)
    plan = list(reversed(late_stages)) + list(reversed(early_stages)) + [
        (key_state, 0, None),
        (prepare, 3, None),
        (middle, early_done, None),
        (local_gradients, early_done + 8, None),
        (last, late_done, None),
    ]

    def turn(t, carry):
        for body, start, condition in plan:
            head = t - start
            ok = (head >= 0) & (head < HEADS)

            @pl.when(ok if condition is None else ok & condition)
            def _(body=body, head=head):
                body(head)

        return carry

    lax.fori_loop(0, late_done + HEADS, turn, 0)
    gq_ref[...] = gq_acc[...].astype(jnp.bfloat16)
    gk_ref[...] = gk_acc[...].astype(jnp.bfloat16)

    def finish(c, carry):
        earlier.finish(c)
        later.finish(c)
        return carry

    lax.fori_loop(0, HEADS, finish, 0)


def deliver(*refs):
    sem = refs[8]
    copies = [pltpu.make_async_copy(refs[i], refs[4 + i], sem.at[i]) for i in range(4)]
    for copy in copies:
        copy.start()
    for copy in copies:
        copy.wait()


def per_device(n_ctx, n_seq, queries, keys, values, grad_output):
    length = queries.shape[0]
    rounds = n_seq.bit_length() - 1
    f32, bf16 = jnp.float32, jnp.bfloat16
    full = pltpu.VMEM((HEADS, 2, ROWS // 2, LANES), f32)
    half = pltpu.VMEM((HEADS, ROWS // 2, LANES), f32)
    halves = pltpu.VMEM((rounds - 1, HEADS, ROWS // 2, LANES), f32)
    semaphores = pltpu.SemaphoreType.DMA((rounds + 3, HEADS))
    scan = [full, full, half, halves, halves, half, full, full, full, full, full]
    scan += [semaphores, semaphores]
    kept = pltpu.VMEM((HEADS, length, HEAD_DIM), f32)
    narrow = pltpu.VMEM((length, LANES), f32)
    vmem = pl.BlockSpec(memory_space=pltpu.VMEM)
    results = pl.pallas_call(
        functools.partial(kernel, n_ctx, n_seq, (1, 2, 1, 2)),
        out_shape=(
            jax.ShapeDtypeStruct(values.shape, bf16),
            jax.ShapeDtypeStruct(queries.shape, bf16),
            jax.ShapeDtypeStruct(keys.shape, bf16),
            jax.ShapeDtypeStruct(values.shape, bf16),
        ),
        in_specs=[vmem] * 8,
        out_specs=(vmem,) * 4,
        scratch_shapes=[narrow, narrow, pltpu.VMEM(values.shape, f32), kept, kept, pltpu.VMEM((HEADS, length, 2 * HEAD_DIM), f32)] + scan + scan,
        compiler_params=pltpu.CompilerParams(
            collective_id=0, has_side_effects=True, vmem_limit_bytes=56 << 20
        ),
        name="attention",
    )(queries, keys, values, grad_output, *tables())
    anywhere = pl.BlockSpec(memory_space=pl.ANY)
    inside = pl.BlockSpec(memory_space=pltpu.VMEM)
    return pl.pallas_call(
        deliver,
        out_shape=tuple(jax.ShapeDtypeStruct(a.shape, a.dtype) for a in results),
        in_specs=[inside] * 4,
        out_specs=(anywhere,) * 4,
        scratch_shapes=[pltpu.SemaphoreType.DMA((4,))],
        name="deliver",
    )(*results)


def solution(mesh):
    placed = P(("seq", "ctx"), None)
    return jax.shard_map(
        functools.partial(per_device, mesh.shape["ctx"], mesh.shape["seq"]),
        mesh=mesh,
        in_specs=(placed,) * 4,
        out_specs=(placed,) * 4,
        check_vma=False,
    )
```
